32 devices in a mesh: aux: 4 (over y, x), occ: 8 (over z, core).
Axes of the slice: x: 2, y: 2, z: 4, core: 2. Of those that a mesh axis runs over, the one named last changes fastest.
Arguments:
- three_index: bfloat16 [2048, 32, 256], P('aux', 'occ'), may hold values from -0.8984375 to 0.8984375
- pair_list: int32 [8, 6], replicated, may hold values from 0 to 7
- pair_counts: int32 [8], replicated, may hold values from 1 to 6, as said below
- domains: int32 [8, 256], replicated, may hold values from 0 to 2047
- pao_energy: float32 [2048], replicated, may hold values from 0.5 to 3
- occ_energy: float32 [32], replicated, may hold values from -2 to -0.3
Outputs:
- density: bfloat16 [2048, 32, 256], P('aux', 'occ')
- pair_energy: float32 [8, 6], P('occ')
The draws below stay inside these ranges and needn't reach their ends.
Inputs may be any that keep to these rules, and one draw needn't show every extreme that they name: `pair_list`: slots at or past a block's count are unused. `pair_counts`: some block uses all 6 slots.
All inputs are finite; a program needn't handle non-finite values.
Results may differ from the reference program's by a relative error of at most 0.0031.
Values may be sent and summed in bfloat16 or wider, within the bound.
No kernel may reach another device: no remote copies, remote signals or barrier semaphores. Data moves between devices by JAX's collectives and lax.ppermute only.
A program may use at most 64 MiB of HBM per device.

```python
import math
import jax
import jax.numpy as jnp
from jax import lax

NAUX = 2048
DOM = 256
OCC_DEV = 4
PMAX = 6
NOB = 8
NOCC = 32
PAOS = 2048


def draw_pair_counts(key, part):
    key_one, key_two = jax.random.split(jax.random.fold_in(key, 17))
    count_draw = jax.random.randint(key_one, (NOB,), 1, PMAX + 1)
    busiest = jax.random.randint(key_two, (), 0, NOB)
    return jnp.where(jnp.arange(NOB) == busiest, PMAX, count_draw).astype(jnp.int32)


def plant(values, rng, low, largest):
    index_at = [jax.random.randint(jax.random.fold_in(rng, axis), (), 0, length) for axis, length in enumerate(values.shape)]
    widest = values.shape.index(max(values.shape))
    beside = index_at[:widest] + [(index_at[widest] + 1) % values.shape[widest]] + index_at[widest + 1:]
    return values.at[tuple(index_at)].set(low).at[tuple(beside)].set(largest)


def shard_levels(rng, extent, cuts, least, largest):
    def one(position, blocks):
        draws = jax.random.uniform(jax.random.fold_in(jax.random.fold_in(rng, 6), position), (blocks,), jnp.float32, least / len(cuts), largest / len(cuts))
        return jnp.repeat(jnp.exp(draws), extent[position] // blocks).reshape((-1,) + (1,) * (len(extent) - position - 1))

    gain = one(*cuts[0])
    for cut in cuts[1:]:
        gain = gain * one(*cut)
    return gain


def bell_draw(own_key, dims, spread, most, pieces=(), held_as=jnp.bfloat16):
    entries = jax.random.normal(own_key, dims, jnp.float32) * spread
    if len(pieces) > 0:
        entries = shard_levels(own_key, dims, pieces, -0.22, 0.18) * entries
    return jnp.clip(entries, min=-most, max=most).astype(held_as)


def setup_inputs(seed: int = 0) -> dict:
    keys = jax.random.split(jax.random.key(seed), 7)
    return {
        "three_index": bell_draw(keys[0], (NAUX, NOCC, DOM), 0.15, 0.8984375, ((0, 4), (1, 8))),
        "pair_list": plant(jax.random.randint(keys[1], (NOB, PMAX), 0, NOB), jax.random.fold_in(keys[1], 1), 0, NOB - 1).astype(jnp.int32),
        "pair_counts": draw_pair_counts(jax.random.fold_in(keys[6], 71), 0),
        "domains": plant(jax.random.randint(keys[3], (NOB, DOM), 0, PAOS), jax.random.fold_in(keys[3], 1), 0, PAOS - 1).astype(jnp.int32),
        "pao_energy": jnp.clip(jnp.exp(jax.random.uniform(keys[4], (PAOS,), jnp.float32, math.log(0.5), math.log(3.0))), 0.5, 3.0),
        "occ_energy": jnp.clip(jax.random.uniform(keys[5], (NOCC,), jnp.float32, -2.0, -0.3), -2.0, -0.3),
    }


def reference(three_index, pair_list, pair_counts, domains, pao_energy, occ_energy):
    pair_rows = OCC_DEV * DOM
    blocks_all = three_index.reshape(NAUX, NOB, pair_rows)
    levels = jnp.take(pao_energy, domains, axis=0)
    occ_levels = occ_energy.reshape(NOB, OCC_DEV)
    denoms = (levels[:, None, :] - occ_levels[:, :, None]).reshape(NOB, pair_rows)

    def one_block(block_id):
        own_block = blocks_all[:, block_id]
        own_denom = denoms[block_id]

        def one_slot(density, slot_id):
            partner_id = pair_list[block_id, slot_id]
            partner = blocks_all[:, partner_id]
            integrals = jnp.dot(own_block.T, partner, preferred_element_type=jnp.float32)
            slot_valid = (slot_id < pair_counts[block_id]).astype(jnp.float32)
            amplitude = (integrals / (own_denom[:, None] + denoms[partner_id][None, :]) * slot_valid).astype(jnp.bfloat16)
            energy = jnp.sum(amplitude.astype(jnp.float32) * integrals) / (pair_rows * pair_rows)
            density = density + jnp.dot(partner, amplitude.T, preferred_element_type=jnp.float32)
            return density, energy

        density, energies = lax.scan(one_slot, jnp.zeros((NAUX, pair_rows), jnp.float32), jnp.arange(PMAX, dtype=jnp.int32))
        return density.astype(jnp.bfloat16), energies

    densities, energies = lax.map(one_block, jnp.arange(NOB, dtype=jnp.int32))
    density_out = jnp.transpose(densities, (1, 0, 2)).reshape(NAUX, NOB * OCC_DEV, DOM)
    return density_out, energies
```

```python
import functools

import jax
import jax.numpy as jnp
from jax import lax
from jax.experimental import pallas as pl
from jax.experimental.pallas import tpu as pltpu
from jax.sharding import PartitionSpec as P


def slot_kernel(part_count, first, last, flags, *refs):
    rows_t, row_denom, col_denom = refs[:3]
    parts = refs[3 : 3 + part_count]
    rest = refs[3 + part_count :]
    if first:
        acc_in, rest = None, rest
    else:
        acc_in, rest = rest[:part_count], rest[part_count:]
    accs, energy = rest[:part_count], rest[part_count]
    depth = parts[0].shape[0]
    integrals = None
    for p in range(part_count):
        term = jnp.dot(
            rows_t[:, p * depth : (p + 1) * depth], parts[p][...], preferred_element_type=jnp.float32
        )
        integrals = term if integrals is None else integrals + term
    amplitude = (integrals / (row_denom[...] + col_denom[...])).astype(jnp.bfloat16)
    energy[...] = jnp.sum(amplitude.astype(jnp.float32) * integrals, axis=0, keepdims=True)[None]
    times = flags[0].astype(jnp.float32)

    def addend(p):
        term = times * lax.dot_general(
            parts[p][...], amplitude, (((1,), (1,)), ((), ())), preferred_element_type=jnp.float32
        )
        return term if first else acc_in[p][...] + term

    half = part_count // 2
    for p in range(part_count):
        value = addend(p)
        if last:
            other = (p + half) % part_count

            @pl.when(flags[1] == 0)
            def _():
                accs[p][...] = value.astype(accs[p].dtype)

            @pl.when(flags[1] != 0)
            def _():
                accs[other][...] = value.astype(accs[other].dtype)
        else:
            accs[p][...] = value


def slot_call(flags, rows_t, row_denom, col_denom, parts, accs, last):
    part_count = len(parts)
    depth, width = parts[0].shape
    rows = rows_t.shape[0]
    block = min(256, rows)
    first = accs is None
    whole = pl.BlockSpec((depth, width), lambda r, f: (0, 0))
    acc_spec = pl.BlockSpec((depth, block), lambda r, f: (0, r))
    in_specs = [
        pl.BlockSpec((block, part_count * depth), lambda r, f: (r, 0)),
        pl.BlockSpec((block, 1), lambda r, f: (r, 0)),
        pl.BlockSpec((1, width), lambda r, f: (0, 0)),
    ] + [whole] * part_count
    operands = [rows_t, row_denom, col_denom] + list(parts)
    aliases = {}
    if not first:
        in_specs += [acc_spec] * part_count
        if not last:
            aliases = {1 + len(operands) + p: p for p in range(part_count)}
        operands += list(accs)
    kinds = [jnp.float32] * part_count
    if last:
        kinds = [jnp.float32] + [jnp.bfloat16] * (part_count - 1)
    flops = 4 * rows * width * depth * part_count
    outs = pl.pallas_call(
        functools.partial(slot_kernel, part_count, first, last),
        grid_spec=pltpu.PrefetchScalarGridSpec(
            num_scalar_prefetch=1,
            grid=(rows // block,),
            in_specs=in_specs,
            out_specs=[acc_spec] * part_count + [pl.BlockSpec((1, 1, width), lambda r, f: (r, 0, 0))],
        ),
        out_shape=[jax.ShapeDtypeStruct((depth, rows), kind) for kind in kinds]
        + [jax.ShapeDtypeStruct((rows // block, 1, width), jnp.float32)],
        input_output_aliases=aliases,
        compiler_params=pltpu.CompilerParams(vmem_limit_bytes=56 * 1024 * 1024),
        cost_estimate=pl.CostEstimate(
            flops=flops, bytes_accessed=2 * part_count * depth * width + 8 * part_count * depth * rows, transcendentals=0
        ),
        name="slot",
    )(flags, *operands)
    return outs[:part_count], jnp.sum(outs[part_count])


def per_device(three_index, pair_list, pair_counts, domains, pao_energy, occ_energy):
    aux_local, occ_dev, dom_width = three_index.shape
    pair_rows = occ_dev * dom_width
    block_count = lax.axis_size("occ")
    block_id = lax.axis_index("occ")
    aux_count = lax.axis_size("aux")
    aux_rank = lax.axis_index("aux")
    slot_total = pair_list.shape[1]
    layers = block_count // 2
    rings = aux_count // 2
    rows = pair_rows // rings
    layer, core = block_id // 2, block_id % 2
    ring, side = aux_rank // 2, aux_rank % 2
    crossed = (core != side).astype(jnp.int32)
    axes = ("aux", "occ")

    def flat(y, x, z, c):
        return (y * 2 + x) * block_count + z * 2 + c

    everyone = [
        (y, x, z, c) for y in range(rings) for x in range(2) for z in range(layers) for c in range(2)
    ]
    swap = [
        (flat(y, x, z, c), flat(y, x, z, c) if c == x else flat(y, 1 - x, z, 1 - c)) for y, x, z, c in everyone
    ]
    lend = [(flat(y, x, z, c), flat(y, 1 - x, z, c)) for y, x, z, c in everyone if c == x]
    down = [(i, (i - 2) % block_count) for i in range(block_count)]
    other_core = [(i, i ^ 1) for i in range(block_count)]

    def to_chip(dy, dx):
        return [(y * 2 + x, ((y + dy) % rings) * 2 + (x ^ dx)) for y in range(rings) for x in range(2)]

    own_block = three_index.reshape(aux_local, pair_rows)
    held = lax.ppermute(own_block, axes, swap)

    levels = jnp.take(pao_energy, domains, axis=0)
    occ_levels = occ_energy.reshape(block_count, occ_dev)
    denoms = (levels[:, None, :] - occ_levels[:, :, None]).reshape(block_count, pair_rows)
    row_denom = lax.dynamic_slice(denoms, (block_id, ring * rows), (1, rows)).reshape(rows, 1)
    my_pairs = pair_list[block_id]
    valid = jnp.arange(slot_total, dtype=jnp.int32) < pair_counts[block_id]

    slots = []
    for k in range(layers):
        if k > 0:
            held = lax.ppermute(held, "occ", down)
        slots.append([held] + [lax.ppermute(held, "aux", to_chip(-dy, 0)) for dy in range(1, rings)])

    energies = jnp.zeros((slot_total,), jnp.float32)
    accs = None
    for k in range(layers):
        mine = slots[k]
        parts = mine + [lax.ppermute(part, "occ", other_core) for part in mine]
        if k == 0:
            local = jnp.concatenate(
                [lax.dynamic_slice(part, (0, ring * rows), (aux_local, rows)) for part in parts], axis=0
            )
            lent = lax.ppermute(local, axes, lend)
            rows_t = jnp.where(crossed == 0, local, lent).T
        partner_id = 2 * ((layer + k) % layers) + side
        hits = (my_pairs == partner_id) & valid
        flags = jnp.stack([jnp.sum(hits.astype(jnp.int32)), crossed])
        col_denom = lax.dynamic_slice(denoms, (partner_id, 0), (1, pair_rows))
        accs, energy = slot_call(flags, rows_t, row_denom, col_denom, parts, accs, k == layers - 1)
        energies = energies + jnp.where(hits, energy / (pair_rows * pair_rows), 0.0)

    slices = []
    for dy in range(rings):
        near, far = accs[dy], lax.ppermute(accs[rings + dy], "aux", to_chip(dy, 1))
        if dy > 0:
            near = lax.ppermute(near, "aux", to_chip(dy, 0))
        slices.append((near.astype(jnp.float32) + far.astype(jnp.float32)).astype(jnp.bfloat16))
    energies = lax.psum(energies, "aux")
    ordered = []
    for i in range(rings):
        chosen = slices[0]
        for dy in range(1, rings):
            chosen = jnp.where((ring - i) % rings == dy, slices[dy], chosen)
        ordered.append(chosen)
    density_out = jnp.concatenate(ordered, axis=1)
    return (density_out.reshape(aux_local, occ_dev, dom_width), energies[None])


def solution(mesh):
    placed = (P("aux", "occ", None), P(), P(), P(), P(), P())
    return jax.shard_map(
        per_device,
        mesh=mesh,
        in_specs=placed,
        out_specs=(P("aux", "occ", None), P("occ", None)),
        check_vma=False,
    )
```

```python
import functools

import jax
import jax.numpy as jnp
from jax import lax
from jax.experimental import pallas as pl
from jax.experimental.pallas import tpu as pltpu
from jax.sharding import PartitionSpec as P


LANES = 128
HALVES = 2


def levels_kernel(table, index, out):
    wanted = index[...]
    lane, row = wanted % LANES, wanted // LANES
    for col in range(wanted.shape[1] // LANES):
        cols = slice(col * LANES, (col + 1) * LANES)
        found = jnp.zeros((wanted.shape[0], LANES), jnp.float32)
        for r in range(table.shape[0]):
            line = jnp.broadcast_to(table[r : r + 1, :], found.shape)
            hit = jnp.take_along_axis(line, lane[:, cols], axis=1)
            found = jnp.where(row[:, cols] == r, hit, found)
        out[:, cols] = found


def slot_kernel(part_count, halves, first, flags, *refs):
    rows_t = refs[:part_count]
    row_denom, col_denom = refs[part_count : part_count + 2]
    rest = refs[part_count + 2 :]
    parts = [rest[h * part_count : (h + 1) * part_count] for h in range(halves)]
    rest = rest[halves * part_count :]
    acc_in = None
    if not first:
        acc_in, rest = rest[:part_count], rest[part_count:]
    accs, energy = rest[:part_count], rest[part_count]
    width = parts[0][0].shape[1]
    amplitudes, energy_sum = [], None
    for h in range(halves):
        integrals = None
        for p in range(part_count):
            term = jnp.dot(rows_t[p][...], parts[h][p][...], preferred_element_type=jnp.float32)
            integrals = term if integrals is None else integrals + term
        denom = row_denom[...] + col_denom[:, h * width : (h + 1) * width]
        amplitude = (integrals / denom).astype(jnp.bfloat16)
        energy_row = jnp.sum(amplitude.astype(jnp.float32) * integrals, axis=0, keepdims=True)
        energy_sum = energy_row if energy_sum is None else energy_sum + energy_row
        amplitudes.append(amplitude)
    energy[...] = energy_sum[None]
    times = flags[0].astype(jnp.float32)
    crossed = flags[1] != 0
    for j in range(part_count):
        other = (j + part_count // 2) % part_count
        term = None
        for h in range(halves):
            block = jnp.where(crossed, parts[h][other][...], parts[h][j][...])
            product = lax.dot_general(
                block, amplitudes[h], (((1,), (1,)), ((), ())), preferred_element_type=jnp.float32
            )
            term = product if term is None else term + product
        term = times * term
        if not first:
            term = acc_in[j][...] + term
        accs[j][...] = term.astype(accs[j].dtype)


def slot_call(flags, rows_t, row_denom, col_denom, parts, accs, last):
    halves, part_count = len(parts), len(parts[0])
    depth, width = parts[0][0].shape
    rows = rows_t.shape[0]
    block = min(256, rows)
    first = accs is None

    def row_map(p):
        return lambda r, f: (r, (p + f[1] * (part_count // 2)) % part_count)

    acc_spec = pl.BlockSpec((depth, block), lambda r, f: (0, r))
    in_specs = [pl.BlockSpec((block, depth), row_map(p)) for p in range(part_count)]
    in_specs += [
        pl.BlockSpec((block, 1), lambda r, f: (r, 0)),
        pl.BlockSpec((1, halves * width), lambda r, f: (0, 0)),
    ]
    in_specs += [pl.BlockSpec((depth, width), lambda r, f: (0, 0))] * (halves * part_count)
    operands = [rows_t] * part_count + [row_denom, col_denom] + [part for half in parts for part in half]
    aliases = {}
    if not first:
        in_specs += [acc_spec] * part_count
        if not last:
            aliases = {1 + len(operands) + p: p for p in range(part_count)}
        operands += list(accs)
    kinds = [jnp.float32] * part_count
    if last:
        kinds = [jnp.float32] + [jnp.bfloat16] * (part_count - 1)
    outs = pl.pallas_call(
        functools.partial(slot_kernel, part_count, halves, first),
        grid_spec=pltpu.PrefetchScalarGridSpec(
            num_scalar_prefetch=1,
            grid=(rows // block,),
            in_specs=in_specs,
            out_specs=[acc_spec] * part_count + [pl.BlockSpec((1, 1, width), lambda r, f: (r, 0, 0))],
        ),
        out_shape=[jax.ShapeDtypeStruct((depth, rows), kind) for kind in kinds]
        + [jax.ShapeDtypeStruct((rows // block, 1, width), jnp.float32)],
        input_output_aliases=aliases,
        compiler_params=pltpu.CompilerParams(vmem_limit_bytes=56 * 1024 * 1024),
        cost_estimate=pl.CostEstimate(
            flops=4 * rows * halves * width * depth * part_count,
            bytes_accessed=2 * part_count * depth * (halves * width + rows) + 8 * part_count * depth * rows,
            transcendentals=0,
        ),
        name="slot",
    )(flags, *operands)
    return outs[:part_count], jnp.sum(outs[part_count])


def per_device(three_index, pair_list, pair_counts, domains, pao_energy, occ_energy):
    aux_local, occ_dev, dom_width = three_index.shape
    pair_rows = occ_dev * dom_width
    width = pair_rows // HALVES
    block_count = lax.axis_size("occ")
    block_id = lax.axis_index("occ")
    aux_count = lax.axis_size("aux")
    aux_rank = lax.axis_index("aux")
    slot_total = pair_list.shape[1]
    layers = block_count // 2
    rings = aux_count // 2
    rows = pair_rows // rings
    layer, core = block_id // 2, block_id % 2
    ring, side = aux_rank // 2, aux_rank % 2
    crossed = (core != side).astype(jnp.int32)
    axes = ("aux", "occ")

    def flat(y, x, z, c):
        return (y * 2 + x) * block_count + z * 2 + c

    everyone = [
        (y, x, z, c) for y in range(rings) for x in range(2) for z in range(layers) for c in range(2)
    ]
    swap = [
        (flat(y, x, z, c), flat(y, x, z, c) if c == x else flat(y, 1 - x, z, 1 - c)) for y, x, z, c in everyone
    ]
    lend = [(flat(y, x, z, c), flat(y, x, z, c) if c == x else flat(y, 1 - x, z, 1 - c)) for y, x, z, c in everyone]
    down = [(i, (i - 2) % block_count) for i in range(block_count)]
    other_core = [(i, i ^ 1) for i in range(block_count)]

    def to_chip(dy, dx):
        return [(y * 2 + x, ((y + dy) % rings) * 2 + (x ^ dx)) for y in range(rings) for x in range(2)]

    halves = range(HALVES)
    own_block = [
        three_index[:, h * occ_dev // HALVES : (h + 1) * occ_dev // HALVES].reshape(aux_local, width) for h in halves
    ]
    held = [[lax.ppermute(own_block[h], axes, swap) for h in halves]]
    for k in range(1, layers):
        held.append([lax.ppermute(held[k - 1][h], "occ", down) for h in halves])
    turned = []
    for k in range(layers):
        turned.append([])
        for h in halves:
            if k == layers - 1 and h == HALVES - 1:
                turned[k].append([lax.ppermute(part, "occ", down) for part in turned[k - 1][h]])
            else:
                turned[k].append([lax.ppermute(held[k][h], "aux", to_chip(-dy, 0)) for dy in range(1, rings)])

    def all_parts(k, h):
        mine = [held[k][h]] + turned[k][h]
        return mine + [lax.ppermute(part, "occ", other_core) for part in mine]

    levels = pl.pallas_call(
        levels_kernel, out_shape=jax.ShapeDtypeStruct(domains.shape, jnp.float32), name="levels"
    )(pao_energy.reshape(-1, LANES), domains)
    occ_levels = occ_energy.reshape(block_count, occ_dev)
    denoms = (levels[:, None, :] - occ_levels[:, :, None]).reshape(block_count, pair_rows)
    row_denom = lax.dynamic_slice(denoms, (block_id, ring * rows), (1, rows)).reshape(rows, 1)
    my_pairs = pair_list[block_id]
    valid = jnp.arange(slot_total, dtype=jnp.int32) < pair_counts[block_id]

    energies = jnp.zeros((slot_total,), jnp.float32)
    accs = None
    rows_t = None
    for k in range(layers):
        parts = [all_parts(k, h) for h in halves]
        if k == 0:
            start = ring * rows
            local = jnp.concatenate(
                [
                    lax.dynamic_slice(
                        jnp.where(start < width, parts[0][p], parts[1][p]), (0, start % width), (aux_local, rows)
                    )
                    for p in range(aux_count)
                ],
                axis=0,
            )
            rows_t = lax.ppermute(local, axes, lend).T
        partner_id = 2 * ((layer + k) % layers) + side
        hits = (my_pairs == partner_id) & valid
        flags = jnp.stack([jnp.sum(hits.astype(jnp.int32)), crossed])
        col_denom = lax.dynamic_slice(denoms, (partner_id, 0), (1, pair_rows))
        if k < layers - 1:
            steps = [(parts, col_denom)]
        else:
            steps = [([parts[h]], col_denom[:, h * width : (h + 1) * width]) for h in halves]
        for i, (step_parts, step_denom) in enumerate(steps):
            last = k == layers - 1 and i == len(steps) - 1
            accs, energy = slot_call(flags, rows_t, row_denom, step_denom, step_parts, accs, last)
            energies = energies + jnp.where(hits, energy / (pair_rows * pair_rows), 0.0)

    slices = []
    for dy in range(rings):
        near, far = accs[dy], lax.ppermute(accs[rings + dy], "aux", to_chip(dy, 1))
        if dy > 0:
            near = lax.ppermute(near, "aux", to_chip(dy, 0))
        slices.append((near.astype(jnp.float32) + far.astype(jnp.float32)).astype(jnp.bfloat16))
    energies = lax.psum(energies, "aux")
    ordered = []
    for i in range(rings):
        chosen = slices[0]
        for dy in range(1, rings):
            chosen = jnp.where((ring - i) % rings == dy, slices[dy], chosen)
        ordered.append(chosen)
    density_out = jnp.concatenate(ordered, axis=1)
    return (density_out.reshape(aux_local, occ_dev, dom_width), energies[None])


def solution(mesh):
    placed = (P("aux", "occ", None), P(), P(), P(), P(), P())

    return jax.shard_map(
        per_device,
        mesh=mesh,
        in_specs=placed,
        out_specs=(P("aux", "occ", None), P("occ", None)),
        check_vma=False,
    )
```

```python
import functools

import jax
import jax.numpy as jnp
from jax import lax
from jax.experimental import pallas as pl
from jax.experimental.pallas import tpu as pltpu
from jax.sharding import PartitionSpec as P


LANES = 128
HALVES = 2


def levels_kernel(table, index, out):
    wanted = index[...]
    lane, row = wanted % LANES, wanted // LANES
    for col in range(wanted.shape[1] // LANES):
        cols = slice(col * LANES, (col + 1) * LANES)
        found = jnp.zeros((wanted.shape[0], LANES), jnp.float32)
        for r in range(table.shape[0]):
            line = jnp.broadcast_to(table[r : r + 1, :], found.shape)
            hit = jnp.take_along_axis(line, lane[:, cols], axis=1)
            found = jnp.where(row[:, cols] == r, hit, found)
        out[:, cols] = found


def slot_kernel(part_count, halves, first, slot, step, block, flags, *refs):
    rows_t = refs[:part_count]
    row_denom, col_denom = refs[part_count : part_count + 2]
    rest = refs[part_count + 2 :]
    parts = [rest[h * part_count : (h + 1) * part_count] for h in range(halves)]
    rest = rest[halves * part_count :]
    acc_in, energy_in = None, None
    if not first:
        acc_in, energy_in, rest = rest[:part_count], rest[part_count], rest[part_count + 1 :]
    accs, energy = rest[:part_count], rest[part_count]
    width = parts[0][0].shape[1]
    times = flags[slot].astype(jnp.float32)
    crossed = flags[flags.shape[0] - 1] != 0
    energy_sum = None
    for start in range(0, rows_t[0].shape[0], block):
        span = slice(start, start + block)
        amplitudes = []
        for h in range(halves):
            integrals = None
            for p in range(part_count):
                term = jnp.dot(rows_t[p][span, :], parts[h][p][...], preferred_element_type=jnp.float32)
                integrals = term if integrals is None else integrals + term
            denom = row_denom[span, :] + col_denom[:, h * width : (h + 1) * width]
            amplitude = (integrals / denom).astype(jnp.bfloat16)
            energy_row = jnp.sum(amplitude.astype(jnp.float32) * integrals, axis=0, keepdims=True)
            energy_sum = energy_row if energy_sum is None else energy_sum + energy_row
            amplitudes.append(amplitude)
        for j in range(part_count):
            other = (j + part_count // 2) % part_count
            term = None
            for h in range(halves):
                block_j = jnp.where(crossed, parts[h][other][...], parts[h][j][...])
                product = lax.dot_general(
                    block_j, amplitudes[h], (((1,), (1,)), ((), ())), preferred_element_type=jnp.float32
                )
                term = product if term is None else term + product
            term = times * term
            if not first:
                term = acc_in[j][:, span] + term
            accs[j][:, span] = term.astype(accs[j].dtype)
    energy[...] = jnp.zeros_like(energy) if first else energy_in[...]
    energy[step : step + 1, :] = energy_sum


def slot_call(flags, slot, step, steps, rows_t, row_denom, col_denom, parts, carry, last):
    halves, part_count = len(parts), len(parts[0])
    depth, width = parts[0][0].shape
    rows = rows_t[0].shape[0]
    first = carry is None
    operands = list(rows_t) + [row_denom, col_denom] + [part for half in parts for part in half]
    aliases = {}
    if not first:
        if not last:
            aliases = {1 + len(operands) + p: p for p in range(part_count + 1)}
        operands += list(carry)
    kinds = [jnp.float32] * part_count
    if last:
        kinds = [jnp.float32] + [jnp.bfloat16] * (part_count - 1)
    in_vmem = pl.BlockSpec(memory_space=pltpu.VMEM)
    return pl.pallas_call(
        functools.partial(slot_kernel, part_count, halves, first, slot, step, min(256, rows)),
        in_specs=[pl.BlockSpec(memory_space=pltpu.SMEM)] + [in_vmem] * len(operands),
        out_specs=[in_vmem] * (part_count + 1),
        out_shape=[jax.ShapeDtypeStruct((depth, rows), kind) for kind in kinds]
        + [jax.ShapeDtypeStruct((steps, width), jnp.float32)],
        input_output_aliases=aliases,
        compiler_params=pltpu.CompilerParams(vmem_limit_bytes=24 * 1024 * 1024),
        cost_estimate=pl.CostEstimate(
            flops=4 * rows * halves * width * depth * part_count,
            bytes_accessed=2 * part_count * depth * (halves * width + rows) + 8 * part_count * depth * rows,
            transcendentals=0,
        ),
        name="slot",
    )(flags, *operands)


def per_device(three_index, pair_list, pair_counts, domains, pao_energy, occ_energy):
    aux_local, occ_dev, dom_width = three_index.shape
    pair_rows = occ_dev * dom_width
    width = pair_rows // HALVES
    block_count = lax.axis_size("occ")
    block_id = lax.axis_index("occ")
    aux_count = lax.axis_size("aux")
    aux_rank = lax.axis_index("aux")
    slot_total = pair_list.shape[1]
    layers = block_count // 2
    rings = aux_count // 2
    rows = pair_rows // rings
    layer, core = block_id // 2, block_id % 2
    ring, side = aux_rank // 2, aux_rank % 2
    crossed = (core != side).astype(jnp.int32)
    axes = ("aux", "occ")

    def flat(y, x, z, c):
        return (y * 2 + x) * block_count + z * 2 + c

    everyone = [
        (y, x, z, c) for y in range(rings) for x in range(2) for z in range(layers) for c in range(2)
    ]
    swap = [
        (flat(y, x, z, c), flat(y, x, z, c) if c == x else flat(y, 1 - x, z, 1 - c)) for y, x, z, c in everyone
    ]
    lend = [(flat(y, x, z, c), flat(y, x, z, c) if c == x else flat(y, 1 - x, z, 1 - c)) for y, x, z, c in everyone]
    down = [(i, (i - 2) % block_count) for i in range(block_count)]
    other_core = [(i, i ^ 1) for i in range(block_count)]

    def to_chip(dy, dx):
        return [(y * 2 + x, ((y + dy) % rings) * 2 + (x ^ dx)) for y in range(rings) for x in range(2)]

    halves = range(HALVES)
    own_block = [
        three_index[:, h * occ_dev // HALVES : (h + 1) * occ_dev // HALVES].reshape(aux_local, width) for h in halves
    ]
    held = [[lax.ppermute(own_block[h], axes, swap) for h in halves]]
    for k in range(1, layers):
        held.append([lax.ppermute(held[k - 1][h], "occ", down) for h in halves])
    turned = []
    for k in range(layers):
        turned.append([])
        for h in halves:
            if k == layers - 1 and h == HALVES - 1:
                turned[k].append([lax.ppermute(part, "occ", down) for part in turned[k - 1][h]])
            else:
                turned[k].append([lax.ppermute(held[k][h], "aux", to_chip(-dy, 0)) for dy in range(1, rings)])

    def all_parts(k, h):
        mine = [held[k][h]] + turned[k][h]
        return mine + [lax.ppermute(part, "occ", other_core) for part in mine]

    levels = pl.pallas_call(
        levels_kernel, out_shape=jax.ShapeDtypeStruct(domains.shape, jnp.float32), name="levels"
    )(pao_energy.reshape(-1, LANES), domains)
    occ_levels = occ_energy.reshape(block_count, occ_dev)
    denoms = (levels[:, None, :] - occ_levels[:, :, None]).reshape(block_count, pair_rows)
    row_denom = lax.dynamic_slice(denoms, (block_id, ring * rows), (1, rows)).reshape(rows, 1)
    my_pairs = pair_list[block_id]
    valid = jnp.arange(slot_total, dtype=jnp.int32) < pair_counts[block_id]

    partner_ids = 2 * ((layer + jnp.arange(layers, dtype=jnp.int32)) % layers) + side
    hits = (my_pairs[None, :] == partner_ids[:, None]) & valid[None, :]
    flags = jnp.concatenate([jnp.sum(hits.astype(jnp.int32), axis=1), crossed[None]])

    start = ring * rows
    parts = [all_parts(0, h) for h in halves]
    rows_t = []
    for p in range(aux_count):
        other = (p + rings) % aux_count
        choices = [jnp.where(crossed == 0, parts[h][p], parts[h][other]) for h in halves]
        piece = jnp.where(start < width, choices[0], choices[1])
        piece = lax.dynamic_slice(piece, (0, start % width), (aux_local, rows))
        rows_t.append(lax.ppermute(piece, axes, lend).T)

    steps = layers - 1 + HALVES
    carry, step_slots = None, []
    for k in range(layers):
        if k > 0:
            parts = [all_parts(k, h) for h in halves]
        col_denom = lax.dynamic_slice(denoms, (2 * ((layer + k) % layers) + side, 0), (1, pair_rows))
        if k < layers - 1:
            pieces = [(parts, col_denom)]
        else:
            pieces = [([parts[h]], col_denom[:, h * width : (h + 1) * width]) for h in halves]
        for step_parts, step_denom in pieces:
            step = len(step_slots)
            step_slots.append(k)
            carry = slot_call(
                flags, k, step, steps, rows_t, row_denom, step_denom, step_parts, carry, step == steps - 1
            )
    accs, energy = carry[:aux_count], carry[aux_count]

    slices = []
    for dy in range(rings):
        near, far = accs[dy], lax.ppermute(accs[rings + dy], "aux", to_chip(dy, 1))
        if dy > 0:
            near = lax.ppermute(near, "aux", to_chip(dy, 0))
        slices.append((near.astype(jnp.float32) + far.astype(jnp.float32)).astype(jnp.bfloat16))
    step_energy = jnp.sum(energy, axis=1) / (pair_rows * pair_rows)
    step_hits = jnp.stack([hits[k] for k in step_slots])
    energies = jnp.sum(jnp.where(step_hits, step_energy[:, None], 0.0), axis=0)
    shares = [lax.ppermute(energies, "aux", to_chip(dy, dx)) for dy in range(rings) for dx in range(2) if dy or dx]
    energies = sum(shares, energies)
    ordered = []
    for i in range(rings):
        chosen = slices[0]
        for dy in range(1, rings):
            chosen = jnp.where((ring - i) % rings == dy, slices[dy], chosen)
        ordered.append(chosen)
    density_out = jnp.concatenate(ordered, axis=1)
    return (density_out.reshape(aux_local, occ_dev, dom_width), energies[None])


def solution(mesh):
    placed = (P("aux", "occ", None), P(), P(), P(), P(), P())

    return jax.shard_map(
        per_device,
        mesh=mesh,
        in_specs=placed,
        out_specs=(P("aux", "occ", None), P("occ", None)),
        check_vma=False,
    )
```
